256 devices in a mesh: blk: 128 (over z, x, y_hi, core), rep: 2 (over y_lo).
Axes of the slice: x: 4, y: 4 (y_hi: 2, y_lo: 2; y = y_hi * 2 + y_lo), z: 8, core: 2. Of those that a mesh axis runs over, the one named last changes fastest.
Arguments:
- block_inputs: bfloat16 [40960, 4096], P(('blk', 'rep')), may hold values from -120 to 120
- out_cotangent: bfloat16 [40960, 4096], P(('blk', 'rep')), may hold values from -6 to 6
- dnormed_in: float32 [40960, 4096], P(('blk', 'rep')), may hold values from -6 to 6
- carried_sums: float32 [3, 14336, 4096], P(None, ('blk', 'rep')), may hold values from -384 to 384
- norm_gain: float32 [4096], replicated, may hold values from 0.1 to 1.9
- w_gate: bfloat16 [7168, 4096], P('blk'), may hold values from -0.09375 to 0.09375
- w_up: bfloat16 [7168, 4096], P('blk'), may hold values from -0.09375 to 0.09375
- w_down: bfloat16 [7168, 4096], P('blk'), may hold values from -0.0625 to 0.0625
Outputs:
- input_grad: bfloat16 [40960, 4096], P(('blk', 'rep'))
- grad_gate: bfloat16 [7168, 4096], P('blk')
- grad_up: bfloat16 [7168, 4096], P('blk')
- grad_down: bfloat16 [7168, 4096], P('blk')
The draws below stay inside these ranges and needn't reach their ends.
All inputs are finite; a program needn't handle non-finite values.
Results may differ from the reference program's by a relative error of at most 0.0038.
Values may be sent and summed in bfloat16 or wider, within the bound.
No kernel may reach another device: no remote copies, remote signals or barrier semaphores. Data moves between devices by JAX's collectives and lax.ppermute only.
A program may use at most 64 MiB of HBM per device.

```python
import math
import jax
import jax.numpy as jnp
from jax import lax

D = 4096
FF_DEV = 56
CYCLE_STEPS = 6
GROUPS = 128
FF = 7168
ROWS = 320
TOKENS = 40960
N_REP = 2


def draw_block_inputs(key, part):
    keys = jax.random.split(jax.random.fold_in(key, 17), 3)
    row_scale = jnp.exp(jax.random.uniform(keys[1], (TOKENS, 1), jnp.float32, 0.0, math.log(10.0)))
    col_scale = jnp.exp(jax.random.uniform(keys[2], (1, D), jnp.float32, math.log(0.3), math.log(3.0)))
    base = jax.random.normal(keys[0], (TOKENS, D), jnp.float32)
    base = jnp.clip(base, -4.0, 4.0)
    return jnp.clip(base * row_scale * col_scale, -120.0, 120.0).astype(jnp.bfloat16)


def levels(stream_key, extent, shards, low, top_value):
    gain = 1.0
    for position, shards_of in shards:
        heights = jax.random.uniform(jax.random.fold_in(jax.random.fold_in(stream_key, 6), position), (shards_of,), jnp.float32, low / len(shards), top_value / len(shards))
        gain = gain * jnp.repeat(jnp.exp(heights), extent[position] // shards_of).reshape((-1,) + (1,) * (len(extent) - 1 - position))
    return gain


def centred(own_key, shape, spread, reach, cuts=(), kind=jnp.bfloat16):
    gain = levels(own_key, shape, cuts, -0.22, 0.18) if cuts else 1.0
    values = jax.random.normal(own_key, shape, jnp.float32) * spread * gain
    return jnp.minimum(jnp.maximum(values, -reach), reach).astype(kind)


def setup_inputs(seed: int = 0) -> dict:
    key_list = jax.random.split(jax.random.key(seed), 9)
    return {
        "block_inputs": draw_block_inputs(jax.random.fold_in(key_list[8], 71), 0),
        "out_cotangent": centred(key_list[1], (TOKENS, D), 1.0, 6.0, ((0, 256),)),
        "dnormed_in": centred(key_list[2], (TOKENS, D), 1.0, 6.0, ((0, 256),), jnp.float32),
        "carried_sums": centred(key_list[3], (3, FF * N_REP, D), (0.3 * (GROUPS * ROWS) ** 0.5), 384.0, ((1, 256),), jnp.float32),
        "norm_gain": jnp.clip(1.0 + 0.18 * jax.random.normal(key_list[4], (D,), jnp.float32), 0.1, 1.9),
        "w_gate": centred(key_list[5], (FF, D), D ** -0.5, 0.09375, ((0, 128),)),
        "w_up": centred(key_list[6], (FF, D), D ** -0.5, 0.09375, ((0, 128),)),
        "w_down": centred(key_list[7], (FF, D), FF ** -0.5, 0.0625, ((0, 128),)),
    }


epsilon = 1e-05

def local_terms(normed, grad_in, gate_rows, up_rows, down_rows):
    gate = jnp.dot(normed, gate_rows.T, preferred_element_type=jnp.float32)
    upper = jnp.dot(normed, up_rows.T, preferred_element_type=jnp.float32)
    sigma = jax.nn.sigmoid(gate)
    act = gate * sigma
    hidden = (act * upper).astype(jnp.bfloat16)
    dhidden = jnp.dot(grad_in, down_rows.T, preferred_element_type=jnp.float32)
    dgate = (dhidden * upper * sigma * (1.0 + gate * (1.0 - sigma))).astype(jnp.bfloat16)
    dup = (dhidden * act).astype(jnp.bfloat16)
    dnormed = jnp.dot(dgate, gate_rows, preferred_element_type=jnp.float32) + jnp.dot(dup, up_rows, preferred_element_type=jnp.float32)
    terms = jnp.stack([jnp.dot(dgate.T, normed, preferred_element_type=jnp.float32), jnp.dot(dup.T, normed, preferred_element_type=jnp.float32), jnp.dot(hidden.T, grad_in, preferred_element_type=jnp.float32)])
    return (terms, dnormed)

def reference(block_inputs, out_cotangent, dnormed_in, carried_sums, norm_gain, w_gate, w_up, w_down):
    scale = 1.0 / math.sqrt(GROUPS * ROWS)
    inputs = block_inputs.reshape(GROUPS, ROWS, D)
    cotangents = out_cotangent.reshape(GROUPS, ROWS, D)
    partials = dnormed_in.reshape(GROUPS, ROWS, D)
    gates = w_gate.reshape(GROUPS, FF_DEV, D)
    uppers = w_up.reshape(GROUPS, FF_DEV, D)
    downs = w_down.reshape(GROUPS, FF_DEV, D)
    held = lax.optimization_barrier(jnp.sum(carried_sums.reshape(3, GROUPS, N_REP, FF_DEV, D), axis=2))
    start_totals = jnp.roll(held, CYCLE_STEPS, axis=1)

    def visit(totals, slot):
        grad_in = lax.dynamic_index_in_dim(cotangents, slot, 0, keepdims=False)
        carried = grad_in.astype(jnp.float32)
        values = lax.dynamic_index_in_dim(inputs, slot, 0, keepdims=False).astype(jnp.float32)
        rstd = lax.rsqrt(lax.optimization_barrier(jnp.mean(values * values, axis=-1, keepdims=True)) + epsilon)
        normed = (values * rstd * norm_gain).astype(jnp.bfloat16)
        dnormed = lax.dynamic_index_in_dim(partials, slot, 0, keepdims=False)
        for step in range(CYCLE_STEPS):
            group = ((slot + CYCLE_STEPS - step) % GROUPS).astype(jnp.int32)
            gate_rows = lax.dynamic_index_in_dim(gates, group, 0, keepdims=False)
            up_rows = lax.dynamic_index_in_dim(uppers, group, 0, keepdims=False)
            down_rows = lax.dynamic_index_in_dim(downs, group, 0, keepdims=False)
            terms, part = local_terms(normed, grad_in, gate_rows, up_rows, down_rows)
            dnormed = dnormed + part
            zero = jnp.int32(0)
            start = (zero, group, zero, zero)
            old = lax.dynamic_slice(totals, start, (3, 1, FF_DEV, D))
            totals = lax.dynamic_update_slice(totals, old + terms[:, None], start)
        scaled = norm_gain * dnormed
        dx = rstd * scaled - values * rstd ** 3 * lax.optimization_barrier(jnp.mean(values * scaled, axis=-1, keepdims=True))
        return (totals, (carried + dx).astype(jnp.bfloat16))
    totals, grads_in = lax.scan(visit, start_totals, jnp.arange(GROUPS, dtype=jnp.int32))
    rounded = (totals * scale).astype(jnp.bfloat16)
    grad_gate = rounded[0].reshape(FF, D)
    grad_up = rounded[1].reshape(FF, D)
    grad_down = rounded[2].reshape(FF, D)
    return (grads_in.reshape(TOKENS, D), grad_gate, grad_up, grad_down)
```

```python
import math

import jax
import jax.numpy as jnp
from jax import lax
from jax.sharding import PartitionSpec as P


AXES = ("blk", "rep")
BF, F32 = jnp.bfloat16, jnp.float32
epsilon = 1e-05


def hop(value, source_of):
    columns = lax.axis_size("blk") // 4
    pairs = []
    for c in range(columns):
        for q in range(2):
            for k in range(2):
                for r in range(2):
                    found = source_of(c, q, k, r)
                    if found is not None:
                        sc, sq, sk, sr = found
                        pairs.append(
                            (((sc % columns) * 4 + sq * 2 + sk) * 2 + sr, (c * 4 + q * 2 + k) * 2 + r)
                        )
    return lax.ppermute(value, AXES, pairs)


def core_swap(c, q, k, r):
    return c, q, 1 - k, r


def rep_swap(c, q, k, r):
    return c, q, k, 1 - r


def cross_swap(c, q, k, r):
    return c, 1 - q, k, 1 - r


def dot(a, b, contract):
    return lax.dot_general(a, b, (contract, ((), ())), preferred_element_type=F32)


def shards(block_inputs, out_cotangent, dnormed_in, carried_sums, norm_gain, w_gate, w_up, w_down):
    rows, width = block_inputs.shape
    units = w_gate.shape[0]
    half = width // 2
    blk, rep = lax.axis_index("blk"), lax.axis_index("rep")
    k, q = blk % 2, (blk // 2) % 2
    h = jnp.bitwise_xor(q, rep)
    scale = 1.0 / math.sqrt(lax.axis_size("blk") * rows * lax.axis_size("rep"))

    def mine(value):
        return lax.dynamic_slice_in_dim(value, h * half, half, value.ndim - 1)

    def other(value):
        return lax.dynamic_slice_in_dim(value, (1 - h) * half, half, value.ndim - 1)

    def joined(own, got):
        return jnp.concatenate([jnp.where(h == 0, own, got), jnp.where(h == 0, got, own)], axis=-1)

    cot_other = hop(other(out_cotangent), rep_swap)
    weights = [mine(w) for w in (w_gate, w_up, w_down)]
    second = [hop(w, lambda c, q, k, r: (c + 1, q, k, r)) for w in weights]
    near = hop(jnp.stack(weights), lambda c, q, k, r: (c, 1, k, 1 - r) if q == 0 else None)
    held = hop(carried_sums.astype(BF), lambda c, q, k, r: (c - 1, q, k, r))
    values = block_inputs.astype(F32)
    rstd = lax.rsqrt(jnp.mean(values * values, axis=-1, keepdims=True) + epsilon)
    normed = (values * rstd * norm_gain).astype(BF)
    norm_other = hop(other(normed), rep_swap)
    cot_mine, norm_mine = mine(out_cotangent), mine(normed)
    cot_mine_p = hop(cot_mine, core_swap)
    norm_mine_p = hop(norm_mine, core_swap)
    crossed = [hop(w, cross_swap) for w in second]
    far = [hop(w, lambda c, q, k, r: (c + 1, 1, k, r) if q == 1 else None) for w in crossed]
    cot_other_p = hop(cot_other, core_swap)
    norm_other_p = hop(norm_other, core_swap)
    held = hop(held, lambda c, q, k, r: (c, 0, k, 1 - r) if q == 1 else (c - 1, 1, k, 1 - r))
    held = mine(held).astype(F32) + hop(other(held), rep_swap).astype(F32)

    norms = (jnp.concatenate([norm_mine, norm_other]), jnp.concatenate([norm_mine_p, norm_other_p]))
    cots = (jnp.concatenate([cot_mine, cot_other]), jnp.concatenate([cot_mine_p, cot_other_p]))
    nt, tn, nn = ((1,), (1,)), ((0,), (0,)), ((1,), (0,))
    sums, met = [], []
    for i, w in enumerate(weights):
        first = jnp.where(q == 0, near[i], crossed[i])
        third = jnp.where(q == 0, crossed[i], far[i])
        both = (
            jnp.concatenate([first, second[i], third]),
            jnp.concatenate([first, second[i], jnp.where(k == 0, third, w)]),
        )
        met.append(both)
        left = norms if i < 2 else cots
        sums.append([dot(left[s], both[s], nt) for s in range(2)])
    held_units = 3 * units
    here = jnp.concatenate([jnp.concatenate([sums[i][s][:rows] for i in range(3)], axis=1) for s in range(2)])
    there = jnp.concatenate([jnp.concatenate([sums[i][s][rows:] for i in range(3)], axis=1) for s in range(2)])
    here = here + hop(there, rep_swap)
    gate = here[:, :held_units]
    upper = here[:, held_units : 2 * held_units]
    dhidden = here[:, 2 * held_units :]
    sigma = jax.nn.sigmoid(gate)
    act = gate * sigma
    hidden = (act * upper).astype(BF)
    dgate = (dhidden * upper * sigma * (1.0 + gate * (1.0 - sigma))).astype(BF)
    dup = (dhidden * act).astype(BF)
    acts = jnp.concatenate([dgate, dup, hidden], axis=1)
    acts_other = hop(acts, rep_swap)
    acts = [jnp.concatenate([acts[s * rows : (s + 1) * rows], acts_other[s * rows : (s + 1) * rows]]) for s in range(2)]

    finals = []
    for i in (2, 0, 1):
        right = norms if i < 2 else cots
        parts = [dot(acts[s][:, i * held_units : (i + 1) * held_units], right[s], tn) for s in range(2)]
        near_sums = parts[0][: 2 * units] + parts[1][: 2 * units]
        own, partner = parts[0][2 * units :], parts[1][2 * units :]
        third_sum = (own + jnp.where(k == 0, partner, 0.0)).astype(BF)
        along = hop(third_sum, lambda c, q, k, r: (c - 1, 1, k, r) if q == 1 else None)
        over = hop(third_sum, lambda c, q, k, r: (c, 0, k, 1 - r) if q == 1 else None)
        first_sum = near_sums[:units] + along.astype(F32)
        swapped = hop(first_sum.astype(BF), cross_swap)
        second_sum = near_sums[units:] + jnp.where(q == 0, swapped, over).astype(F32)
        home = hop(second_sum.astype(BF), lambda c, q, k, r: (c - 1, q, k, r)).astype(F32)
        total = held[i] + home + jnp.where(k == 1, partner, 0.0) + jnp.where(q == 1, swapped.astype(F32), 0.0)
        final = (total * scale).astype(BF)
        finals.append(joined(final, hop(final, rep_swap)))

    back = [
        dot(acts[s][:, :held_units], met[0][s], nn) + dot(acts[s][:, held_units : 2 * held_units], met[1][s], nn)
        for s in range(2)
    ]
    back = back[0] + hop(back[1], core_swap)
    back_got = hop(back[rows:].astype(BF), rep_swap).astype(F32)
    dnormed = dnormed_in + joined(back[:rows], back_got)
    scaled = norm_gain * dnormed
    dx = rstd * scaled - values * rstd**3 * jnp.mean(values * scaled, axis=-1, keepdims=True)
    input_grad = (out_cotangent.astype(F32) + dx).astype(BF)
    return (input_grad, finals[1], finals[2], finals[0])


def solution(mesh):
    placed = (
        P(("blk", "rep"), None),
        P(("blk", "rep"), None),
        P(("blk", "rep"), None),
        P(None, ("blk", "rep"), None),
        P(),
        P("blk", None),
        P("blk", None),
        P("blk", None),
    )

    def step(*args):
        return shards(*args)

    step = jax.shard_map(
        step,
        mesh=mesh,
        in_specs=placed,
        out_specs=(P(("blk", "rep"), None), P("blk", None), P("blk", None), P("blk", None)),
        check_vma=False,
    )
    return step
```

```python
import functools
import math

import jax
import jax.numpy as jnp
from jax import lax
from jax.experimental import pallas as pl
from jax.experimental.pallas import tpu as pltpu
from jax.sharding import PartitionSpec as P


AXES = ("blk", "rep")
BF, F32 = jnp.bfloat16, jnp.float32
epsilon = 1e-05


def hop(value, source_of):
    columns = lax.axis_size("blk") // 4
    pairs = []
    for c in range(columns):
        for q in range(2):
            for k in range(2):
                for r in range(2):
                    found = source_of(c, q, k, r)
                    if found is not None:
                        sc, sq, sk, sr = found
                        pairs.append(
                            (((sc % columns) * 4 + sq * 2 + sk) * 2 + sr, (c * 4 + q * 2 + k) * 2 + r)
                        )
    return lax.ppermute(value, AXES, pairs)


def core_swap(c, q, k, r):
    return c, q, 1 - k, r


def rep_swap(c, q, k, r):
    return c, q, k, 1 - r


def cross_swap(c, q, k, r):
    return c, 1 - q, k, 1 - r


def dot(a, b, contract):
    return lax.dot_general(a, b, (contract, ((), ())), preferred_element_type=F32)


def scores_kernel(count, core, x_own, x_par, *refs):
    first, second, third, held_here = (refs[count * i : count * (i + 1)] for i in range(4))
    rows, units = x_own.shape[0], first[0].shape[0]
    tokens = jnp.concatenate([x_own[...], x_par[...]], axis=0)
    got = []
    for f, s, t, w in zip(first, second, third, held_here):
        last = jnp.where(core[0] == 0, t[...], w[...])
        out = dot(tokens, jnp.concatenate([f[...], s[...], t[...], last], axis=0), ((1,), (1,)))
        got.append(out[:rows, : 3 * units])
        got += [out[rows:, : 2 * units], out[rows:, 3 * units :]]
    refs[-1][...] = jnp.concatenate(got, axis=1)


def in_vmem(count):
    return [pl.BlockSpec(memory_space=pltpu.VMEM)] * count


def scores(core, x_own, x_par, sets, picked):
    rows, half = x_own.shape
    columns = 6 * len(picked) * sets[0][0].shape[0]
    return pl.pallas_call(
        functools.partial(scores_kernel, len(picked)),
        out_shape=jax.ShapeDtypeStruct((rows, columns), F32),
        in_specs=[pl.BlockSpec(memory_space=pltpu.SMEM)] + in_vmem(2 + 4 * len(picked)),
        out_specs=in_vmem(1)[0],
        cost_estimate=pl.CostEstimate(
            flops=2 * rows * columns * half, bytes_accessed=4 * rows * half + 2 * columns * half, transcendentals=0
        ),
    )(core, x_own, x_par, *(group[i] for group in sets for i in picked))


def back_kernel(core, acts_mine, acts_other, *refs):
    sets, outs = [x[...] for x in refs[:8]], refs[8:]
    units = sets[0].shape[0]
    span = 3 * units
    last = [jnp.where(core[0] == 0, sets[4 + i], sets[6 + i]) for i in range(2)]
    for s, tail in enumerate((sets[4:6], last)):
        met = jnp.concatenate([x for i in range(2) for x in (sets[i], sets[2 + i], tail[i])], axis=0)
        for o, acts in enumerate((acts_other, acts_mine)):
            value = acts[...]
            lhs = jnp.concatenate(
                [value[:, span * s : span * (s + 1)], value[:, span * (2 + s) : span * (3 + s)]], axis=1
            )
            outs[2 * s + o][...] = dot(lhs, met, ((1,), (0,)))


def back_sums(core, acts_mine, acts_other, sets):
    rows = acts_mine.shape[0]
    units, half = sets[0][0].shape
    return pl.pallas_call(
        back_kernel,
        out_shape=[jax.ShapeDtypeStruct((rows, half), F32)] * 4,
        in_specs=[pl.BlockSpec(memory_space=pltpu.SMEM)] + in_vmem(10),
        out_specs=in_vmem(4),
        name="back",
        cost_estimate=pl.CostEstimate(
            flops=48 * rows * units * half, bytes_accessed=16 * rows * half + 16 * units * half, transcendentals=0
        ),
    )(core, acts_mine, acts_other, *(group[i] for group in sets for i in range(2)))


def gradient_kernel(i, core, acts_mine, acts_other, t_mine, t_other, t_mine_p, t_other_p, *outs):
    third_out, first_out, second_out, home_out = outs
    rows, half = t_mine.shape
    units = third_out.shape[0]
    even = core[0] == 0
    span = 3 * units
    lhs = []
    for acts in (acts_mine, acts_other):
        value = acts[...].astype(F32)[:, 2 * span * i : 2 * span * (i + 1)]
        none = jnp.zeros((rows, units), F32)
        lhs.append(jnp.concatenate([value[:, :span], none], axis=1))
        lhs.append(jnp.concatenate([value[:, span : span + 2 * units], none, value[:, span + 2 * units :]], axis=1))
    lhs = jnp.transpose(jnp.concatenate(lhs, axis=0)).astype(BF)
    step = 512
    for at in range(0, half, step):
        cols = slice(at, at + step)
        tokens = jnp.concatenate([t[:, cols] for t in (t_mine, t_mine_p, t_other, t_other_p)], axis=0)
        out = dot(lhs, tokens, ((1,), (0,)))
        first_out[:, cols] = out[:units]
        second_out[:, cols] = out[units : 2 * units]
        last = out[3 * units :]
        third_out[:, cols] = (out[2 * units : 3 * units] + jnp.where(even, last, 0.0)).astype(BF)
        home_out[:, cols] = jnp.where(even, 0.0, last)


def gradient(i, core, acts_mine, acts_other, tokens, units):
    rows, half = tokens[0].shape
    vmem = pl.BlockSpec(memory_space=pltpu.VMEM)
    return pl.pallas_call(
        functools.partial(gradient_kernel, i),
        out_shape=[jax.ShapeDtypeStruct((units, half), kind) for kind in (BF, F32, F32, F32)],
        in_specs=[pl.BlockSpec(memory_space=pltpu.SMEM)] + [vmem] * 6,
        out_specs=[vmem] * 4,
        cost_estimate=pl.CostEstimate(
            flops=24 * rows * units * half, bytes_accessed=8 * rows * half + 14 * units * half, transcendentals=0
        ),
    )(core, acts_mine, acts_other, *tokens)


def shards(block_inputs, out_cotangent, dnormed_in, carried_sums, norm_gain, w_gate, w_up, w_down):
    rows, width = block_inputs.shape
    units = w_gate.shape[0]
    half = width // 2
    blk, rep = lax.axis_index("blk"), lax.axis_index("rep")
    k, q = blk % 2, (blk // 2) % 2
    h = jnp.bitwise_xor(q, rep)
    scale = 1.0 / math.sqrt(lax.axis_size("blk") * rows * lax.axis_size("rep"))

    def mine(value):
        return lax.dynamic_slice_in_dim(value, h * half, half, value.ndim - 1)

    def other(value):
        return lax.dynamic_slice_in_dim(value, (1 - h) * half, half, value.ndim - 1)

    def joined(own, got):
        return jnp.concatenate([jnp.where(h == 0, own, got), jnp.where(h == 0, got, own)], axis=-1)

    cot_other = hop(other(out_cotangent), rep_swap)
    weights = [mine(w) for w in (w_gate, w_up, w_down)]
    weights = list(lax.optimization_barrier(tuple(weights)))
    second = [hop(w, lambda c, q, k, r: (c + 1, q, k, r)) for w in weights]
    held = hop(carried_sums.astype(BF), lambda c, q, k, r: (c - 1, q, k, r))
    values = block_inputs.astype(F32)
    rstd = lax.rsqrt(jnp.mean(values * values, axis=-1, keepdims=True) + epsilon)
    normed = (values * rstd * norm_gain).astype(BF)
    norm_other = hop(other(normed), rep_swap)
    cot_mine, norm_mine = mine(out_cotangent), mine(normed)
    cot_mine_p = hop(cot_mine, core_swap)
    norm_mine_p = hop(norm_mine, core_swap)
    first = [hop(jnp.where(q == 0, s, w), cross_swap) for s, w in zip(second, weights)]
    third = [hop(w, lambda c, q, k, r: (c + 1, q, k, r)) for w in first]
    cot_other_p = hop(cot_other, core_swap)
    norm_other_p = hop(norm_other, core_swap)
    held = hop(held, lambda c, q, k, r: (c, 0, k, 1 - r) if q == 1 else (c - 1, 1, k, 1 - r))
    held = mine(held).astype(F32) + hop(other(held), rep_swap).astype(F32)

    held_units = 3 * units
    core = jnp.full((1,), k, jnp.int32)
    sets = (first, second, third, weights)
    dhidden = scores(core, cot_other, cot_other_p, sets, (2,))
    got = hop(dhidden, rep_swap)
    dhidden = scores(core, cot_mine, cot_mine_p, sets, (2,)) + got
    pre = scores(core, norm_other, norm_other_p, sets, (0, 1))
    got = hop(pre, rep_swap)
    pre = scores(core, norm_mine, norm_mine_p, sets, (0, 1)) + got
    gate, upper = pre[:, : 2 * held_units], pre[:, 2 * held_units :]
    sigma = jax.nn.sigmoid(gate)
    act = gate * sigma
    hidden = (act * upper).astype(BF)
    hidden_other = hop(hidden, rep_swap)
    dgate = (dhidden * upper * sigma * (1.0 + gate * (1.0 - sigma))).astype(BF)
    dup = (dhidden * act).astype(BF)
    acts = jnp.concatenate([dgate, dup], axis=1)
    acts_other = hop(acts, rep_swap)

    norms = (norm_mine, norm_other, norm_mine_p, norm_other_p)
    cots = (cot_mine, cot_other, cot_mine_p, cot_other_p)
    finals = []
    for i in (2, 0, 1):
        third_sum, first_sum, second_sum, home_sum = gradient(
            *((i, core, acts, acts_other, norms) if i < 2 else (0, core, hidden, hidden_other, cots)), units
        )
        along = hop(third_sum, lambda c, q, k, r: (c - 1, q, k, r))
        swapped = hop((first_sum + along.astype(F32)).astype(BF), cross_swap).astype(F32)
        second_sum = second_sum + jnp.where(q == 0, swapped, 0.0)
        home = hop(second_sum.astype(BF), lambda c, q, k, r: (c - 1, q, k, r)).astype(F32)
        total = held[i] + home + home_sum + jnp.where(q == 1, swapped, 0.0)
        final = (total * scale).astype(BF)
        finals.append((final, hop(final, rep_swap)))

    own_other, own_mine, par_other, par_mine = back_sums(core, acts, acts_other, sets)
    back_other = own_other + hop(par_other, core_swap)
    back_got = hop(back_other.astype(BF), rep_swap).astype(F32)
    back_mine = own_mine + hop(par_mine, core_swap)
    dnormed = dnormed_in + joined(back_mine, back_got)
    scaled = norm_gain * dnormed
    dx = rstd * scaled - values * rstd**3 * jnp.mean(values * scaled, axis=-1, keepdims=True)
    input_grad = (out_cotangent.astype(F32) + dx).astype(BF)
    finals = [joined(final, lax.optimization_barrier((got, input_grad))[0]) for final, got in finals]
    return (input_grad, finals[1], finals[2], finals[0])


def solution(mesh):
    placed = (
        P(("blk", "rep"), None),
        P(("blk", "rep"), None),
        P(("blk", "rep"), None),
        P(None, ("blk", "rep"), None),
        P(),
        P("blk", None),
        P("blk", None),
        P("blk", None),
    )

    def step(*args):
        return shards(*args)

    step = jax.shard_map(
        step,
        mesh=mesh,
        in_specs=placed,
        out_specs=(P(("blk", "rep"), None), P("blk", None), P("blk", None), P("blk", None)),
        check_vma=False,
    )
    return step
```

```python
import functools
import math

import jax
import jax.numpy as jnp
from jax import lax
from jax.experimental import pallas as pl
from jax.experimental.pallas import tpu as pltpu
from jax.sharding import PartitionSpec as P


AXES = ("blk", "rep")
BF, F32 = jnp.bfloat16, jnp.float32
epsilon = 1e-05


def hop(value, source_of):
    columns = lax.axis_size("blk") // 4
    pairs = []
    for c in range(columns):
        for q in range(2):
            for k in range(2):
                for r in range(2):
                    found = source_of(c, q, k, r)
                    if found is not None:
                        sc, sq, sk, sr = found
                        pairs.append(
                            (((sc % columns) * 4 + sq * 2 + sk) * 2 + sr, (c * 4 + q * 2 + k) * 2 + r)
                        )
    return lax.ppermute(value, AXES, pairs)


def core_swap(c, q, k, r):
    return c, q, 1 - k, r


def rep_swap(c, q, k, r):
    return c, q, k, 1 - r


def cross_swap(c, q, k, r):
    return c, 1 - q, k, 1 - r


def dot(a, b, contract):
    return lax.dot_general(a, b, (contract, ((), ())), preferred_element_type=F32)


def scores_kernel(count, core, x_own, x_par, *refs):
    first, second, third, held_here = (refs[count * i : count * (i + 1)] for i in range(4))
    rows, units = x_own.shape[0], first[0].shape[0]
    tokens = jnp.concatenate([x_own[...], x_par[...]], axis=0)
    got = []
    for f, s, t, w in zip(first, second, third, held_here):
        last = jnp.where(core[0] == 0, t[...], w[...])
        out = dot(tokens, jnp.concatenate([f[...], s[...], t[...], last], axis=0), ((1,), (1,)))
        got.append(out[:rows, : 3 * units])
        got += [out[rows:, : 2 * units], out[rows:, 3 * units :]]
    refs[-1][...] = jnp.concatenate(got, axis=1)


def in_vmem(count):
    return [pl.BlockSpec(memory_space=pltpu.VMEM)] * count


def scores(core, x_own, x_par, sets, picked):
    rows, half = x_own.shape
    columns = 6 * len(picked) * sets[0][0].shape[0]
    return pl.pallas_call(
        functools.partial(scores_kernel, len(picked)),
        out_shape=jax.ShapeDtypeStruct((rows, columns), F32),
        in_specs=[pl.BlockSpec(memory_space=pltpu.SMEM)] + in_vmem(2 + 4 * len(picked)),
        out_specs=in_vmem(1)[0],
        cost_estimate=pl.CostEstimate(
            flops=2 * rows * columns * half, bytes_accessed=4 * rows * half + 2 * columns * half, transcendentals=0
        ),
    )(core, x_own, x_par, *(group[i] for group in sets for i in picked))


def back_kernel(core, acts_mine, acts_other, *refs):
    sets, outs = [x[...] for x in refs[:8]], refs[8:]
    units = sets[0].shape[0]
    span = 3 * units
    last = [jnp.where(core[0] == 0, sets[4 + i], sets[6 + i]) for i in range(2)]
    for s, tail in enumerate((sets[4:6], last)):
        met = jnp.concatenate([x for i in range(2) for x in (sets[i], sets[2 + i], tail[i])], axis=0)
        for o, acts in enumerate((acts_other, acts_mine)):
            value = acts[...]
            lhs = jnp.concatenate(
                [value[:, span * s : span * (s + 1)], value[:, span * (2 + s) : span * (3 + s)]], axis=1
            )
            got = dot(lhs, met, ((1,), (0,)))
            if s == 0:
                outs[o][...] = got
            else:
                outs[2][o * lhs.shape[0] : (o + 1) * lhs.shape[0], :] = got.astype(BF)


def back_sums(core, acts_mine, acts_other, sets):
    rows = acts_mine.shape[0]
    units, half = sets[0][0].shape
    return pl.pallas_call(
        back_kernel,
        out_shape=[jax.ShapeDtypeStruct((rows, half), F32)] * 2 + [jax.ShapeDtypeStruct((2 * rows, half), BF)],
        in_specs=[pl.BlockSpec(memory_space=pltpu.SMEM)] + in_vmem(10),
        out_specs=in_vmem(3),
        name="back",
        cost_estimate=pl.CostEstimate(
            flops=48 * rows * units * half, bytes_accessed=16 * rows * half + 16 * units * half, transcendentals=0
        ),
    )(core, acts_mine, acts_other, *(group[i] for group in sets for i in range(2)))


def gradient_kernel(i, core, acts_mine, acts_other, t_mine, t_other, t_mine_p, t_other_p, *outs):
    third_out, first_out, second_out, home_out = outs
    rows, half = t_mine.shape
    units = third_out.shape[0]
    even = core[0] == 0
    span = 3 * units
    lhs = []
    for acts in (acts_mine, acts_other):
        value = acts[...].astype(F32)[:, 2 * span * i : 2 * span * (i + 1)]
        none = jnp.zeros((rows, units), F32)
        lhs.append(jnp.concatenate([value[:, :span], none], axis=1))
        lhs.append(jnp.concatenate([value[:, span : span + 2 * units], none, value[:, span + 2 * units :]], axis=1))
    lhs = jnp.transpose(jnp.concatenate(lhs, axis=0)).astype(BF)
    step = 512
    for at in range(0, half, step):
        cols = slice(at, at + step)
        tokens = jnp.concatenate([t[:, cols] for t in (t_mine, t_mine_p, t_other, t_other_p)], axis=0)
        out = dot(lhs, tokens, ((1,), (0,)))
        first_out[:, cols] = out[:units]
        second_out[:, cols] = out[units : 2 * units]
        last = out[3 * units :]
        third_out[:, cols] = (out[2 * units : 3 * units] + jnp.where(even, last, 0.0)).astype(BF)
        home_out[:, cols] = jnp.where(even, 0.0, last)


def gradient(i, core, acts_mine, acts_other, tokens, units):
    rows, half = tokens[0].shape
    vmem = pl.BlockSpec(memory_space=pltpu.VMEM)
    return pl.pallas_call(
        functools.partial(gradient_kernel, i),
        out_shape=[jax.ShapeDtypeStruct((units, half), kind) for kind in (BF, F32, F32, F32)],
        in_specs=[pl.BlockSpec(memory_space=pltpu.SMEM)] + [vmem] * 6,
        out_specs=[vmem] * 4,
        cost_estimate=pl.CostEstimate(
            flops=24 * rows * units * half, bytes_accessed=8 * rows * half + 14 * units * half, transcendentals=0
        ),
    )(core, acts_mine, acts_other, *tokens)


def shards(block_inputs, out_cotangent, dnormed_in, carried_sums, norm_gain, w_gate, w_up, w_down):
    rows, width = block_inputs.shape
    units = w_gate.shape[0]
    half = width // 2
    blk, rep = lax.axis_index("blk"), lax.axis_index("rep")
    k, q = blk % 2, (blk // 2) % 2
    h = jnp.bitwise_xor(q, rep)
    scale = 1.0 / math.sqrt(lax.axis_size("blk") * rows * lax.axis_size("rep"))

    def mine(value):
        return lax.dynamic_slice_in_dim(value, h * half, half, value.ndim - 1)

    def other(value):
        return lax.dynamic_slice_in_dim(value, (1 - h) * half, half, value.ndim - 1)

    def joined(own, got):
        return jnp.concatenate([jnp.where(h == 0, own, got), jnp.where(h == 0, got, own)], axis=-1)

    cot_other = hop(other(out_cotangent), rep_swap)
    weights = [mine(w) for w in (w_gate, w_up, w_down)]
    weights = list(lax.optimization_barrier(tuple(weights)))
    second = [hop(w, lambda c, q, k, r: (c + 1, q, k, r)) for w in weights]
    held = hop(carried_sums.astype(BF), lambda c, q, k, r: (c - 1, q, k, r))
    values = block_inputs.astype(F32)
    rstd = lax.rsqrt(jnp.mean(values * values, axis=-1, keepdims=True) + epsilon)
    normed = (values * rstd * norm_gain).astype(BF)
    norm_other = hop(other(normed), rep_swap)
    cot_mine, norm_mine = mine(out_cotangent), mine(normed)
    cot_mine_p = hop(cot_mine, core_swap)
    norm_mine_p = hop(norm_mine, core_swap)
    first = [hop(jnp.where(q == 0, s, w), cross_swap) for s, w in zip(second, weights)]
    third = [hop(w, lambda c, q, k, r: (c + 1, q, k, r)) for w in first]
    cot_other_p = hop(cot_other, core_swap)
    norm_other_p = hop(norm_other, core_swap)
    held = hop(held, lambda c, q, k, r: (c, 0, k, 1 - r) if q == 1 else (c - 1, 1, k, 1 - r))
    held = mine(held).astype(F32) + hop(other(held), rep_swap).astype(F32)

    held_units = 3 * units
    core = jnp.full((1,), k, jnp.int32)
    sets = (first, second, third, weights)
    dhidden = scores(core, cot_other, cot_other_p, sets, (2,))
    got = hop(dhidden, rep_swap)
    dhidden = scores(core, cot_mine, cot_mine_p, sets, (2,)) + got
    pre = scores(core, norm_other, norm_other_p, sets, (0, 1))
    got = hop(pre, rep_swap)
    pre = scores(core, norm_mine, norm_mine_p, sets, (0, 1)) + got
    gate, upper = pre[:, : 2 * held_units], pre[:, 2 * held_units :]
    sigma = jax.nn.sigmoid(gate)
    act = gate * sigma
    hidden = (act * upper).astype(BF)
    hidden_other = hop(hidden, rep_swap)
    dgate = (dhidden * upper * sigma * (1.0 + gate * (1.0 - sigma))).astype(BF)
    dup = (dhidden * act).astype(BF)
    acts = jnp.concatenate([dgate, dup], axis=1)
    acts_other = hop(acts, rep_swap)

    norms = (norm_mine, norm_other, norm_mine_p, norm_other_p)
    cots = (cot_mine, cot_other, cot_mine_p, cot_other_p)
    finals = []
    for i in (2, 0, 1):
        third_sum, first_sum, second_sum, home_sum = gradient(
            *((i, core, acts, acts_other, norms) if i < 2 else (0, core, hidden, hidden_other, cots)), units
        )
        along = hop(third_sum, lambda c, q, k, r: (c - 1, q, k, r))
        swapped = hop((first_sum + along.astype(F32)).astype(BF), cross_swap).astype(F32)
        second_sum = second_sum + jnp.where(q == 0, swapped, 0.0)
        home = hop(second_sum.astype(BF), lambda c, q, k, r: (c - 1, q, k, r)).astype(F32)
        if finals:
            home = lax.optimization_barrier((home, finals[-1][0]))[0]
        total = held[i] + home + home_sum + jnp.where(q == 1, swapped, 0.0)
        final = (total * scale).astype(BF)
        finals.append((final, hop(final, rep_swap)))

    own_other, own_mine, partner = back_sums(core, acts, acts_other, sets)
    partner = hop(partner, core_swap)
    back_got = hop((own_other + partner[:rows].astype(F32)).astype(BF), rep_swap).astype(F32)
    back_mine = own_mine + partner[rows:].astype(F32)
    dnormed = dnormed_in + joined(back_mine, back_got)
    scaled = norm_gain * dnormed
    dx = rstd * scaled - values * rstd**3 * jnp.mean(values * scaled, axis=-1, keepdims=True)
    input_grad = (out_cotangent.astype(F32) + dx).astype(BF)
    for n, (final, got) in enumerate(finals):
        finals[n] = joined(final, lax.optimization_barrier((got, input_grad))[0])
    return (input_grad, finals[1], finals[2], finals[0])


def solution(mesh):
    placed = (
        P(("blk", "rep"), None),
        P(("blk", "rep"), None),
        P(("blk", "rep"), None),
        P(None, ("blk", "rep"), None),
        P(),
        P("blk", None),
        P("blk", None),
        P("blk", None),
    )

    def step(*args):
        return shards(*args)

    step = jax.shard_map(
        step,
        mesh=mesh,
        in_specs=placed,
        out_specs=(P(("blk", "rep"), None), P("blk", None), P("blk", None), P("blk", None)),
        check_vma=False,
    )
    return step
```

```python
import functools
import math

import jax
import jax.numpy as jnp
from jax import lax
from jax.experimental import pallas as pl
from jax.experimental.pallas import tpu as pltpu
from jax.sharding import PartitionSpec as P


AXES = ("blk", "rep")
BF, F32 = jnp.bfloat16, jnp.float32
epsilon = 1e-05


def hop(value, source_of):
    columns = lax.axis_size("blk") // 4
    pairs = []
    for c in range(columns):
        for q in range(2):
            for k in range(2):
                for r in range(2):
                    found = source_of(c, q, k, r)
                    if found is not None:
                        sc, sq, sk, sr = found
                        pairs.append(
                            (((sc % columns) * 4 + sq * 2 + sk) * 2 + sr, (c * 4 + q * 2 + k) * 2 + r)
                        )
    return lax.ppermute(value, AXES, pairs)


def core_swap(c, q, k, r):
    return c, q, 1 - k, r


def rep_swap(c, q, k, r):
    return c, q, k, 1 - r


def cross_swap(c, q, k, r):
    return c, 1 - q, k, 1 - r


def dot(a, b, contract):
    return lax.dot_general(a, b, (contract, ((), ())), preferred_element_type=F32)


def scores_kernel(count, core, x_own, x_par, *refs):
    first, second, third, held_here = (refs[count * i : count * (i + 1)] for i in range(4))
    rows, units = x_own.shape[0], first[0].shape[0]
    tokens = jnp.concatenate([x_own[...], x_par[...]], axis=0)
    got = []
    for f, s, t, w in zip(first, second, third, held_here):
        last = jnp.where(core[0] == 0, t[...], w[...])
        out = dot(tokens, jnp.concatenate([f[...], s[...], t[...], last], axis=0), ((1,), (1,)))
        got.append(out[:rows, : 3 * units])
        got += [out[rows:, : 2 * units], out[rows:, 3 * units :]]
    refs[-1][...] = jnp.concatenate(got, axis=1)


def in_vmem(count):
    return [pl.BlockSpec(memory_space=pltpu.VMEM)] * count


def scores(core, x_own, x_par, sets, picked):
    rows, half = x_own.shape
    columns = 6 * len(picked) * sets[0][0].shape[0]
    return pl.pallas_call(
        functools.partial(scores_kernel, len(picked)),
        out_shape=jax.ShapeDtypeStruct((rows, columns), F32),
        in_specs=[pl.BlockSpec(memory_space=pltpu.SMEM)] + in_vmem(2 + 4 * len(picked)),
        out_specs=in_vmem(1)[0],
        cost_estimate=pl.CostEstimate(
            flops=2 * rows * columns * half, bytes_accessed=4 * rows * half + 2 * columns * half, transcendentals=0
        ),
    )(core, x_own, x_par, *(group[i] for group in sets for i in picked))


def back_kernel(core, acts_mine, acts_other, *refs):
    sets, outs = [x[...] for x in refs[:8]], refs[8:]
    units = sets[0].shape[0]
    span = 3 * units
    last = [jnp.where(core[0] == 0, sets[4 + i], sets[6 + i]) for i in range(2)]
    for s, tail in enumerate((sets[4:6], last)):
        met = jnp.concatenate([x for i in range(2) for x in (sets[i], sets[2 + i], tail[i])], axis=0)
        for o, acts in enumerate((acts_other, acts_mine)):
            value = acts[...]
            lhs = jnp.concatenate(
                [value[:, span * s : span * (s + 1)], value[:, span * (2 + s) : span * (3 + s)]], axis=1
            )
            got = dot(lhs, met, ((1,), (0,)))
            if s == 0:
                outs[o][...] = got
            else:
                outs[2][o * lhs.shape[0] : (o + 1) * lhs.shape[0], :] = got.astype(BF)


def back_sums(core, acts_mine, acts_other, sets):
    rows = acts_mine.shape[0]
    units, half = sets[0][0].shape
    return pl.pallas_call(
        back_kernel,
        out_shape=[jax.ShapeDtypeStruct((rows, half), F32)] * 2 + [jax.ShapeDtypeStruct((2 * rows, half), BF)],
        in_specs=[pl.BlockSpec(memory_space=pltpu.SMEM)] + in_vmem(10),
        out_specs=in_vmem(3),
        name="back",
        cost_estimate=pl.CostEstimate(
            flops=48 * rows * units * half, bytes_accessed=16 * rows * half + 16 * units * half, transcendentals=0
        ),
    )(core, acts_mine, acts_other, *(group[i] for group in sets for i in range(2)))


def gradient_kernel(core, acts_mine, acts_other, t_mine, t_other, t_mine_p, t_other_p, *outs):
    units, half = outs[0].shape
    rows, span = t_mine.shape[0], 3 * units
    arrays = len(outs) // 4
    even = core[0] == 0
    none = jnp.zeros((rows, units), F32)
    lhs = []
    for acts in (acts_mine, acts_other):
        value = acts[...].astype(F32)
        own, partner = [], []
        for i in range(arrays):
            part = value[:, 2 * span * i : 2 * span * (i + 1)]
            own += [part[:, :span], none]
            partner += [part[:, span : span + 2 * units], none, part[:, span + 2 * units :]]
        lhs += [jnp.concatenate(own, axis=1), jnp.concatenate(partner, axis=1)]
    lhs = jnp.transpose(jnp.concatenate(lhs, axis=0)).astype(BF)
    step = 512 // arrays
    for at in range(0, half, step):
        cols = slice(at, at + step)
        tokens = jnp.concatenate([t[:, cols] for t in (t_mine, t_mine_p, t_other, t_other_p)], axis=0)
        both = dot(lhs, tokens, ((1,), (0,)))
        for i in range(arrays):
            third_out, first_out, second_out, home_out = outs[4 * i : 4 * i + 4]
            out = both[4 * units * i : 4 * units * (i + 1)]
            first_out[:, cols] = out[:units]
            second_out[:, cols] = out[units : 2 * units]
            last = out[3 * units :]
            third_out[:, cols] = (out[2 * units : 3 * units] + jnp.where(even, last, 0.0)).astype(BF)
            home_out[:, cols] = jnp.where(even, 0.0, last)


def gradient(core, acts_mine, acts_other, tokens, units):
    rows, half = tokens[0].shape
    arrays = acts_mine.shape[1] // (6 * units)
    return pl.pallas_call(
        gradient_kernel,
        out_shape=[jax.ShapeDtypeStruct((units, half), kind) for kind in (BF, F32, F32, F32)] * arrays,
        in_specs=[pl.BlockSpec(memory_space=pltpu.SMEM)] + in_vmem(6),
        out_specs=in_vmem(4 * arrays),
        cost_estimate=pl.CostEstimate(
            flops=32 * arrays * rows * units * half,
            bytes_accessed=8 * rows * half + 14 * arrays * units * half,
            transcendentals=0,
        ),
    )(core, acts_mine, acts_other, *tokens)


def shards(block_inputs, out_cotangent, dnormed_in, carried_sums, norm_gain, w_gate, w_up, w_down):
    rows, width = block_inputs.shape
    units = w_gate.shape[0]
    half = width // 2
    blk, rep = lax.axis_index("blk"), lax.axis_index("rep")
    k, q = blk % 2, (blk // 2) % 2
    h = jnp.bitwise_xor(q, rep)
    scale = 1.0 / math.sqrt(lax.axis_size("blk") * rows * lax.axis_size("rep"))

    def mine(value):
        return lax.dynamic_slice_in_dim(value, h * half, half, value.ndim - 1)

    def other(value):
        return lax.dynamic_slice_in_dim(value, (1 - h) * half, half, value.ndim - 1)

    def joined(own, got):
        return jnp.concatenate([jnp.where(h == 0, own, got), jnp.where(h == 0, got, own)], axis=-1)

    cot_other = hop(other(out_cotangent), rep_swap)
    weights = [mine(w) for w in (w_gate, w_up, w_down)]
    weights = list(lax.optimization_barrier(tuple(weights)))
    second = [hop(w, lambda c, q, k, r: (c + 1, q, k, r)) for w in weights]
    held = hop(carried_sums.astype(BF), lambda c, q, k, r: (c - 1, q, k, r))
    values = block_inputs.astype(F32)
    rstd = lax.rsqrt(jnp.mean(values * values, axis=-1, keepdims=True) + epsilon)
    normed = (values * rstd * norm_gain).astype(BF)
    norm_other = hop(other(normed), rep_swap)
    cot_mine, norm_mine = mine(out_cotangent), mine(normed)
    cot_mine_p = hop(cot_mine, core_swap)
    norm_mine_p = hop(norm_mine, core_swap)
    first = [hop(jnp.where(q == 0, s, w), cross_swap) for s, w in zip(second, weights)]
    third = [hop(w, lambda c, q, k, r: (c + 1, q, k, r)) for w in first]
    cot_other_p = hop(cot_other, core_swap)
    norm_other_p = hop(norm_other, core_swap)
    held = hop(held, lambda c, q, k, r: (c, 0, k, 1 - r) if q == 1 else (c - 1, 1, k, 1 - r))
    held = mine(held).astype(F32) + hop(other(held), rep_swap).astype(F32)

    held_units = 3 * units
    core = jnp.full((1,), k, jnp.int32)
    sets = (first, second, third, weights)
    dhidden = scores(core, cot_other, cot_other_p, sets, (2,))
    got = hop(dhidden, rep_swap)
    dhidden = scores(core, cot_mine, cot_mine_p, sets, (2,)) + got
    pre = scores(core, norm_other, norm_other_p, sets, (0, 1))
    got = hop(pre, rep_swap)
    pre = scores(core, norm_mine, norm_mine_p, sets, (0, 1)) + got
    gate, upper = pre[:, : 2 * held_units], pre[:, 2 * held_units :]
    sigma = jax.nn.sigmoid(gate)
    act = gate * sigma
    hidden = (act * upper).astype(BF)
    hidden_other = hop(hidden, rep_swap)
    dgate = (dhidden * upper * sigma * (1.0 + gate * (1.0 - sigma))).astype(BF)
    dup = (dhidden * act).astype(BF)
    acts = jnp.concatenate([dgate, dup], axis=1)
    acts_other = hop(acts, rep_swap)

    norms = (norm_mine, norm_other, norm_mine_p, norm_other_p)
    cots = (cot_mine, cot_other, cot_mine_p, cot_other_p)
    finals = []
    sums = gradient(core, hidden, hidden_other, cots, units)
    sums += gradient(core, acts, acts_other, norms, units)
    for n, i in enumerate((2, 0, 1)):
        third_sum, first_sum, second_sum, home_sum = sums[4 * n : 4 * n + 4]
        along = hop(third_sum, lambda c, q, k, r: (c - 1, q, k, r))
        if i == 2:
            along = lax.optimization_barrier((along, sums[4]))[0]
        swapped = hop((first_sum + along.astype(F32)).astype(BF), cross_swap).astype(F32)
        second_sum = second_sum + jnp.where(q == 0, swapped, 0.0)
        home = hop(second_sum.astype(BF), lambda c, q, k, r: (c - 1, q, k, r)).astype(F32)
        if finals:
            home = lax.optimization_barrier((home, finals[-1][0]))[0]
        total = held[i] + home + home_sum + jnp.where(q == 1, swapped, 0.0)
        final = (total * scale).astype(BF)
        finals.append((final, hop(final, rep_swap)))

    own_other, own_mine, partner = back_sums(core, acts, acts_other, sets)
    partner = hop(partner, core_swap)
    back_got = hop((own_other + partner[:rows].astype(F32)).astype(BF), rep_swap).astype(F32)
    back_mine = own_mine + partner[rows:].astype(F32)
    dnormed = dnormed_in + joined(back_mine, back_got)
    scaled = norm_gain * dnormed
    dx = rstd * scaled - values * rstd**3 * jnp.mean(values * scaled, axis=-1, keepdims=True)
    input_grad = (out_cotangent.astype(F32) + dx).astype(BF)
    for n, (final, got) in enumerate(finals):
        finals[n] = joined(final, lax.optimization_barrier((got, input_grad))[0])
    return (input_grad, finals[1], finals[2], finals[0])


def solution(mesh):
    placed = (
        P(("blk", "rep"), None),
        P(("blk", "rep"), None),
        P(("blk", "rep"), None),
        P(None, ("blk", "rep"), None),
        P(),
        P("blk", None),
        P("blk", None),
        P("blk", None),
    )

    def step(*args):
        return shards(*args)

    step = jax.shard_map(
        step,
        mesh=mesh,
        in_specs=placed,
        out_specs=(P(("blk", "rep"), None), P("blk", None), P("blk", None), P("blk", None)),
        check_vma=False,
    )
    return step
```
